512 devices in a mesh: seq: 128 (over x, y, z_lo), head: 4 (over z_hi, core).
Axes of the slice: x: 4, y: 4, z: 16 (z_hi: 2, z_lo: 8; z = z_hi * 8 + z_lo), core: 2. Of those that a mesh axis runs over, the one named last changes fastest.
Arguments:
- queries: bfloat16 [65536, 4096], P('seq', 'head'), may hold values from -80 to 80
- keys_next: bfloat16 [65536, 1024], P('seq', 'head'), may hold values from -4 to 4
- values_next: bfloat16 [65536, 1024], P('seq', 'head'), may hold values from -6 to 6
- keys_front: bfloat16 [1024, 1024], P(None, 'head'), may hold values from -4 to 4
- values_front: bfloat16 [1024, 1024], P(None, 'head'), may hold values from -6 to 6
- keys_prev: bfloat16 [65536, 1024], P('seq', 'head'), may hold values from -6 to 6
- values_prev: bfloat16 [65536, 1024], P('seq', 'head'), may hold values from -6 to 6
Outputs:
- attended: bfloat16 [65536, 4096], P('seq', 'head')
- banded_keys: bfloat16 [65536, 1024], P('seq', 'head')
- banded_values: bfloat16 [65536, 1024], P('seq', 'head')
The draws below stay inside these ranges and needn't reach their ends.
All inputs are finite; a program needn't handle non-finite values.
Results may differ from the reference program's by a relative error of at most 0.0075.
Values may be sent and summed in bfloat16 or wider, within the bound.
No kernel may reach another device: no remote copies, remote signals or barrier semaphores. Data moves between devices by JAX's collectives and lax.ppermute only.
A program may use at most 64 MiB of HBM per device.

```python
import jax
import jax.numpy as jnp
from jax import lax

QH = 32
KVH = 8
HD = 128
TOK_DEV = 512
TOKENS = 65536
N_SEQ = 128


def shared_draw(key):
    keys_raw = jnp.clip(jax.random.normal(jax.random.fold_in(key, 11), (TOKENS, KVH, HD), jnp.float32), -4.0, 4.0)
    query_raw = jnp.clip(jax.random.normal(jax.random.fold_in(key, 12), (TOKENS, QH, HD), jnp.float32), -4.0, 4.0)
    return (query_raw.reshape(TOKENS, QH * HD), keys_raw.reshape(TOKENS, KVH * HD))


def draw_queries(key, part):
    return shared_draw(key)[0].astype(jnp.bfloat16)


def draw_keys_next(key, part):
    return shared_draw(key)[1].astype(jnp.bfloat16)


def shard_levels(rng, dims, shards, least, top_value):
    loudness = 1.0
    for axis_at, blocks in shards:
        heights = jax.random.uniform(jax.random.fold_in(jax.random.fold_in(rng, 6), axis_at), (blocks,), jnp.float32, least / len(shards), top_value / len(shards))
        loudness = loudness * jnp.repeat(jnp.exp(heights), dims[axis_at] // blocks).reshape((-1,) + (1,) * (len(dims) - 1 - axis_at))
    return loudness


def noise(rng, extent, scale, bound, split=(), kind=jnp.bfloat16):
    drawn = jax.random.normal(rng, extent, jnp.float32) * scale
    if len(split) > 0:
        drawn = shard_levels(rng, extent, split, -0.22, 0.18) * drawn
    return jnp.clip(drawn, min=-bound, max=bound).astype(kind)


def setup_inputs(seed: int = 0) -> dict:
    seeds = jax.random.split(jax.random.key(seed), 8)
    queries = draw_queries(jax.random.fold_in(seeds[7], 71), 0)
    keys_next = draw_keys_next(jax.random.fold_in(seeds[7], 71), 0)
    values_next = noise(seeds[2], (TOKENS, KVH * HD), 1.0, 6.0, ((0, 128), (1, 4)))
    keys_front = noise(seeds[3], (2 * TOK_DEV, KVH * HD), 1.0, 4.0, ((1, 4),))
    values_front = noise(seeds[4], (2 * TOK_DEV, KVH * HD), 1.0, 6.0, ((1, 4),))
    keys_prev = noise(seeds[5], (TOKENS, KVH * HD), 1.0, 6.0, ((0, 128), (1, 4)))
    values_prev = noise(seeds[6], (TOKENS, KVH * HD), 1.0, 6.0, ((0, 128), (1, 4)))
    return dict(queries=queries, keys_next=keys_next, values_next=values_next, keys_front=keys_front, values_front=values_front, keys_prev=keys_prev, values_prev=values_prev)


def block_attention(query_rows, keys_window, values_window, first_query, first_key):
    ratio = QH // KVH
    shaped = query_rows.reshape(TOK_DEV, KVH, ratio, HD).astype(jnp.float32)
    keys_f = keys_window.reshape(3 * TOK_DEV, KVH, HD).astype(jnp.float32)
    scores = jnp.einsum('sgrd,tgd->grst', shaped, keys_f) * (HD ** -0.5)
    query_pos = first_query + jnp.arange(TOK_DEV, dtype=jnp.int32)
    key_pos = first_key + jnp.arange(3 * TOK_DEV, dtype=jnp.int32)
    visible = key_pos[None, :] <= query_pos[:, None]
    masked = jnp.where(visible, scores, -jnp.inf)
    top = jnp.max(masked, axis=-1, keepdims=True)
    mass = jnp.where(visible, jnp.exp(masked - top), 0.0)
    total = jnp.sum(mass, axis=-1)
    weights = mass.astype(jnp.bfloat16).astype(jnp.float32)
    values_f = values_window.reshape(3 * TOK_DEV, KVH, HD).astype(jnp.float32)
    summed = jnp.einsum('grst,tgd->grsd', weights, values_f)
    result = summed / total[..., None]
    return jnp.transpose(result, (2, 0, 1, 3)).reshape(TOK_DEV, QH * HD).astype(jnp.bfloat16)


def reference(queries, keys_next, values_next, keys_front, values_front, keys_prev, values_prev):
    width = KVH * HD
    keys_pad = jnp.concatenate([keys_front, keys_next], axis=0)
    values_pad = jnp.concatenate([values_front, values_next], axis=0)

    def one_block(block):
        start = (block * TOK_DEV).astype(jnp.int32)
        query_rows = lax.dynamic_slice_in_dim(queries, start, TOK_DEV, 0)
        keys_window = lax.dynamic_slice_in_dim(keys_pad, start, 3 * TOK_DEV, 0)
        values_window = lax.dynamic_slice_in_dim(values_pad, start, 3 * TOK_DEV, 0)
        return block_attention(query_rows, keys_window, values_window, start, start - 2 * TOK_DEV)

    blocks = lax.map(one_block, jnp.arange(N_SEQ, dtype=jnp.int32))
    attended = blocks.reshape(TOKENS, QH * HD)
    banded_keys = keys_prev.reshape(TOK_DEV, N_SEQ, width).transpose(1, 0, 2).reshape(TOKENS, width)
    banded_values = values_prev.reshape(TOK_DEV, N_SEQ, width).transpose(1, 0, 2).reshape(TOKENS, width)
    return attended, banded_keys, banded_values
```

```python
import functools

import jax
import jax.numpy as jnp
from jax import lax
from jax.experimental import pallas as pl
from jax.experimental.pallas import tpu as pltpu
from jax.sharding import PartitionSpec as P


QH = 32
KVH = 8
HD = 128
RATIO = QH // KVH
ROWS = 512
WIDTH = 256
HEADS = 8
NZ = 8
NXY = 16
EXP_SCALE = 1.4426950408889634 * HD**-0.5
HALF = 256

XY_GROUPS = [[z + NZ * c for c in range(NXY)] for z in range(NZ)]
Z_GROUPS = [[NZ * c + z for z in range(NZ)] for c in range(NXY)]


def shifted(value):
    count = lax.axis_size("seq")
    return lax.ppermute(value, "seq", [(source, source + 1) for source in range(count - 1)])


def vmem():
    return pl.BlockSpec(memory_space=pltpu.VMEM)


def anywhere():
    return pl.BlockSpec(memory_space=pl.ANY)


def smem():
    return pl.BlockSpec(memory_space=pltpu.SMEM)


def cost(flops, moved):
    return pl.CostEstimate(flops=flops, bytes_accessed=moved, transcendentals=0)


def pack_kernel(keys_ref, values_ref, out_ref, sems):
    copies = []
    for kv, ref in enumerate((keys_ref, values_ref)):
        for k in range(4):
            copies.append(
                pltpu.make_async_copy(
                    ref.at[k], out_ref.at[:, pl.ds(kv * 32 + k * 8, 8), :], sems.at[kv * 4 + k]
                )
            )
    for copy in copies:
        copy.start()
    for copy in copies:
        copy.wait()


def pack(keys, values):
    return pl.pallas_call(
        pack_kernel,
        out_shape=jax.ShapeDtypeStruct((NXY, 64, WIDTH), jnp.bfloat16),
        in_specs=[anywhere(), anywhere()],
        out_specs=vmem(),
        scratch_shapes=[pltpu.SemaphoreType.DMA((8,))],
        cost_estimate=cost(0, 1 << 20),
        name="pack",
    )(keys.reshape(4, NXY, 8, WIDTH), values.reshape(4, NXY, 8, WIDTH))


def chooser(source_of_row):
    row = lax.broadcasted_iota(jnp.int32, (128, 128), 0)
    col = lax.broadcasted_iota(jnp.int32, (128, 128), 1)
    return jnp.where(col == source_of_row(row), 1.0, 0.0).astype(jnp.bfloat16)


def middle_kernel(x_ref, out_ref):
    pick = chooser(lambda r: (r & 15) * 8 + (r >> 4))
    for kv in range(2):
        for c in range(4):
            rows = jnp.concatenate(
                [x_ref[c * 4 + s, pl.ds(kv * 32, 32), :] for s in range(4)], axis=0
            )
            moved = jnp.dot(pick, rows, preferred_element_type=jnp.float32).astype(jnp.bfloat16)
            for z in range(NZ):
                out_ref[z, pl.ds(kv * 64 + c * 16, 16), :] = moved[z * 16 : (z + 1) * 16, :]


def middle(x):
    return pl.pallas_call(
        middle_kernel,
        out_shape=jax.ShapeDtypeStruct((NZ, 128, WIDTH), jnp.bfloat16),
        in_specs=[vmem()],
        out_specs=vmem(),
        cost_estimate=cost(1 << 26, 1 << 20),
        name="middle",
    )(x)


def final_kernel(x_ref, keys_ref, values_ref):
    pick = chooser(lambda r: ((r >> 2) & 7) * 16 + (r >> 5) * 4 + (r & 3))
    for kv, ref in enumerate((keys_ref, values_ref)):
        for c in range(4):
            rows = jnp.concatenate(
                [x_ref[z, pl.ds(kv * 64 + c * 16, 16), :] for z in range(NZ)], axis=0
            )
            moved = jnp.dot(pick, rows, preferred_element_type=jnp.float32)
            ref[pl.ds(c * 128, 128), :] = moved.astype(jnp.bfloat16)


def final(x):
    shape = jax.ShapeDtypeStruct((ROWS, WIDTH), jnp.bfloat16)
    return pl.pallas_call(
        final_kernel,
        out_shape=(shape, shape),
        in_specs=[vmem()],
        out_specs=(vmem(), vmem()),
        cost_estimate=cost(1 << 26, 1 << 20),
        name="final",
    )(x)


def scores_of(q, keys):
    return lax.dot_general(
        q, keys, (((1,), (1,)), ((), ())), preferred_element_type=jnp.float32
    )


def fetch(choices, keys_buf, values_buf, sems):
    for when, keys_src, values_src in choices:

        @pl.when(when)
        def _(keys_src=keys_src, values_src=values_src):
            keys_copy = pltpu.make_async_copy(keys_src, keys_buf, sems.at[0])
            values_copy = pltpu.make_async_copy(values_src, values_buf, sems.at[1])
            keys_copy.start()
            values_copy.start()
            keys_copy.wait()
            values_copy.wait()


def head_slices(h):
    mine = pl.ds(pl.multiple_of(h * HD, HD), HD)
    group = pl.ds(pl.multiple_of((h // RATIO) * HD, HD), HD)
    return mine, group


def near_kernel(
    pos_ref, q_ref, k0_ref, v0_ref, k1_ref, v1_ref, kf_ref, vf_ref,
    o_ref, m_ref, l_ref, k_buf, v_buf, sems,
):
    pos = pos_ref[0]
    late = pl.ds(ROWS, ROWS)
    fetch(
        ((pos == 0, kf_ref.at[late], vf_ref.at[late]), (pos != 0, k1_ref, v1_ref)),
        k_buf, v_buf, sems,
    )
    lane = lax.broadcasted_iota(jnp.int32, (HALF, 128), 1)
    row = lax.broadcasted_iota(jnp.int32, (HALF, HALF), 0)
    col = lax.broadcasted_iota(jnp.int32, (HALF, HALF), 1)
    visible = col <= row

    def body(h, carry):
        mine, group = head_slices(h)
        for i in range(ROWS // HALF):
            span = pl.ds(i * HALF, HALF)
            q = q_ref[span, mine]
            parts = [(scores_of(q, k_buf[:, group]), v_buf[:, group])]
            if i > 0:
                before = pl.ds(0, i * HALF)
                parts.append((scores_of(q, k0_ref[before, group]), v0_ref[before, group]))
            own = scores_of(q, k0_ref[span, group])
            parts.append((jnp.where(visible, own, -jnp.inf), v0_ref[span, group]))
            top = functools.reduce(
                jnp.maximum, [jnp.max(s, axis=1, keepdims=True) for s, _ in parts]
            )
            total = jnp.zeros((HALF, 1), jnp.float32)
            summed = jnp.zeros((HALF, HD), jnp.float32)
            for s, values in parts:
                mass = jnp.exp2((s - top) * EXP_SCALE)
                total += jnp.sum(mass, axis=1, keepdims=True)
                summed += jnp.dot(
                    mass.astype(jnp.bfloat16), values, preferred_element_type=jnp.float32
                )
            o_ref[span, mine] = summed
            m_ref[span, :] = jnp.where(lane == h, top, m_ref[span, :])
            l_ref[span, :] = jnp.where(lane == h, total, l_ref[span, :])
        return carry

    m_ref[...] = jnp.zeros_like(m_ref)
    l_ref[...] = jnp.zeros_like(l_ref)
    lax.fori_loop(0, HEADS, body, 0)


def near(pos, q, k0, v0, k1, v1, kf, vf):
    stat = jax.ShapeDtypeStruct((ROWS, 128), jnp.float32)
    return pl.pallas_call(
        near_kernel,
        out_shape=(jax.ShapeDtypeStruct((ROWS, HEADS * HD), jnp.float32), stat, stat),
        in_specs=[smem(), vmem(), vmem(), vmem(), anywhere(), anywhere(), anywhere(), anywhere()],
        out_specs=(vmem(), vmem(), vmem()),
        scratch_shapes=[
            pltpu.VMEM((ROWS, WIDTH), jnp.bfloat16),
            pltpu.VMEM((ROWS, WIDTH), jnp.bfloat16),
            pltpu.SemaphoreType.DMA((2,)),
        ],
        cost_estimate=cost(3 << 30, 5 << 20),
        name="near",
    )(pos, q, k0, v0, k1, v1, kf, vf)


def far_kernel(
    pos_ref, q_ref, k2_ref, v2_ref, kf_ref, vf_ref, o_ref, m_ref, l_ref,
    out_ref, k_buf, v_buf, sems,
):
    pos = pos_ref[0]
    early = pl.ds(0, ROWS)
    late = pl.ds(ROWS, ROWS)
    fetch(
        (
            (pos == 0, kf_ref.at[early], vf_ref.at[early]),
            (pos == 1, kf_ref.at[late], vf_ref.at[late]),
            (pos > 1, k2_ref, v2_ref),
        ),
        k_buf, v_buf, sems,
    )
    lane = lax.broadcasted_iota(jnp.int32, (HALF, 128), 1)

    def body(h, carry):
        mine, group = head_slices(h)
        for i in range(ROWS // HALF):
            span = pl.ds(i * HALF, HALF)
            s = scores_of(q_ref[span, mine], k_buf[:, group])
            old_top = jnp.sum(jnp.where(lane == h, m_ref[span, :], 0.0), axis=1, keepdims=True)
            old_total = jnp.sum(jnp.where(lane == h, l_ref[span, :], 0.0), axis=1, keepdims=True)
            top = jnp.maximum(jnp.max(s, axis=1, keepdims=True), old_top)
            mass = jnp.exp2((s - top) * EXP_SCALE)
            keep = jnp.exp2((old_top - top) * EXP_SCALE)
            total = keep * old_total + jnp.sum(mass, axis=1, keepdims=True)
            summed = keep * o_ref[span, mine] + jnp.dot(
                mass.astype(jnp.bfloat16), v_buf[:, group], preferred_element_type=jnp.float32
            )
            out_ref[span, mine] = (summed / total).astype(jnp.bfloat16)
        return carry

    lax.fori_loop(0, HEADS, body, 0)


def far(pos, q, k2, v2, kf, vf, o, m, l):
    return pl.pallas_call(
        far_kernel,
        out_shape=jax.ShapeDtypeStruct((ROWS, HEADS * HD), jnp.bfloat16),
        in_specs=[smem(), vmem(), anywhere(), anywhere(), anywhere(), anywhere(), vmem(), vmem(), vmem()],
        out_specs=vmem(),
        scratch_shapes=[
            pltpu.VMEM((ROWS, WIDTH), jnp.bfloat16),
            pltpu.VMEM((ROWS, WIDTH), jnp.bfloat16),
            pltpu.SemaphoreType.DMA((2,)),
        ],
        cost_estimate=cost(2 << 30, 5 << 20),
        name="far",
    )(pos, q, k2, v2, kf, vf, o, m, l)


def exchange(x, groups):
    return lax.all_to_all(
        x, "seq", split_axis=0, concat_axis=0, tiled=True, axis_index_groups=groups
    )


def shards(queries, keys_next, values_next, keys_front, values_front, keys_prev, values_prev):
    pos = lax.axis_index("seq").astype(jnp.int32).reshape(1)
    k1 = shifted(keys_next)
    v1 = shifted(values_next)
    k2 = shifted(k1)
    v2 = shifted(v1)
    packed = pack(keys_prev, values_prev)
    crossed = exchange(packed, XY_GROUPS)
    mixed = middle(crossed)
    arrived = exchange(mixed, Z_GROUPS)
    state = near(pos, queries, keys_next, values_next, k1, v1, keys_front, values_front)
    attended = far(pos, queries, k2, v2, keys_front, values_front, *state)
    banded_keys, banded_values = final(arrived)
    return (attended, banded_keys, banded_values)


def solution(mesh):
    in_specs = (
        P("seq", "head"),
        P("seq", "head"),
        P("seq", "head"),
        P(None, "head"),
        P(None, "head"),
        P("seq", "head"),
        P("seq", "head"),
    )
    out_specs = (P("seq", "head"), P("seq", "head"), P("seq", "head"))
    return jax.shard_map(
        shards, mesh=mesh, in_specs=in_specs, out_specs=out_specs, check_vma=False
    )
```

```python
import functools

import jax
import jax.numpy as jnp
from jax import lax
from jax.experimental import pallas as pl
from jax.experimental.pallas import tpu as pltpu
from jax.sharding import PartitionSpec as P


QH = 32
KVH = 8
HD = 128
RATIO = QH // KVH
ROWS = 512
WIDTH = 256
HEADS = 8
EXP_SCALE = 1.4426950408889634 * HD**-0.5
NEAR = 256
FAR = 256
LIMIT = 24 << 20


def shifted(value):
    count = lax.axis_size("seq")
    return lax.ppermute(value, "seq", [(source, source + 1) for source in range(count - 1)])


def vmem():
    return pl.BlockSpec(memory_space=pltpu.VMEM)


def anywhere():
    return pl.BlockSpec(memory_space=pl.ANY)


def smem():
    return pl.BlockSpec(memory_space=pltpu.SMEM)


def cost(flops, moved):
    return pl.CostEstimate(flops=flops, bytes_accessed=moved, transcendentals=0)


def chooser(size, source_of_row):
    row = lax.broadcasted_iota(jnp.int32, (size, size), 0)
    col = lax.broadcasted_iota(jnp.int32, (size, size), 1)
    return jnp.where(col == source_of_row(row), 1.0, 0.0).astype(jnp.bfloat16)


def moved_by(pick, parts):
    rows = jnp.concatenate(parts, axis=0) if len(parts) > 1 else parts[0]
    return jnp.dot(pick, rows, preferred_element_type=jnp.float32).astype(jnp.bfloat16)


def pack_kernel(k_ref, v_ref, out_ref):
    pick = chooser(128, lambda r: (r & 7) * 16 + (r >> 3))
    for c in range(8):
        out_ref[pl.ds(c * 128, 128), :] = moved_by(
            pick, [ref[pl.ds(k * 128 + c * 16, 16), :] for ref in (k_ref, v_ref) for k in range(4)])


def pack(keys, values):
    packed = pl.pallas_call(
        pack_kernel,
        out_shape=jax.ShapeDtypeStruct((2 * ROWS, WIDTH), jnp.bfloat16),
        in_specs=[vmem(), vmem()],
        out_specs=vmem(),
        cost_estimate=cost(1 << 26, 1 << 20),
        name="pack",
    )(keys, values)
    return packed.reshape(ROWS // 4, 8, WIDTH)


def unpack_kernel(x_ref, k_ref, v_ref):
    pick = chooser(128, lambda r: ((r >> 2) & 15) * 8 + (r >> 6) * 4 + (r & 3))
    for c in range(8):
        moved = moved_by(pick, [x_ref[pl.ds(c * 128, 128), :]])
        k_ref[pl.ds(c * 64, 64), :] = moved[:64]
        v_ref[pl.ds(c * 64, 64), :] = moved[64:]


def unpack(x):
    shape = jax.ShapeDtypeStruct((ROWS, WIDTH), jnp.bfloat16)
    return pl.pallas_call(
        unpack_kernel,
        out_shape=(shape, shape),
        in_specs=[vmem()],
        out_specs=(vmem(), vmem()),
        compiler_params=pltpu.CompilerParams(vmem_limit_bytes=8 << 20),
        cost_estimate=cost(1 << 26, 1 << 20),
        name="unpack",
    )(x.reshape(2 * ROWS, WIDTH))


def exchange(x):
    return lax.all_to_all(
        x, "seq", split_axis=0, concat_axis=0, tiled=True
    )


def scores_of(q, keys):
    return lax.dot_general(
        q, keys, (((1,), (1,)), ((), ())), preferred_element_type=jnp.float32
    )


def fetch(choices, keys_buf, wide_buf, sems):
    for when, keys_src, values_src in choices:

        @pl.when(when)
        def _(keys_src=keys_src, values_src=values_src):
            copies = [pltpu.make_async_copy(keys_src, keys_buf, sems.at[0])]
            for g in range(2):
                copies.append(
                    pltpu.make_async_copy(
                        values_src.at[:, pl.ds(g * HD, HD)],
                        wide_buf.at[g, :, pl.ds(0, HD)],
                        sems.at[1 + g],
                    )
                )
            for copy in copies:
                copy.start()
            for copy in copies:
                copy.wait()


def set_ones(wide_buf):
    for g in range(2):
        wide_buf[g, :, HD:] = jnp.ones_like(wide_buf[g, :, HD:])


def near_kernel(
    pos_ref, q_ref, k0_ref, v0_ref, k1_ref, v1_ref, kf_ref, vf_ref,
    o_ref, m_ref, l_ref, k_buf, wide1, wide0, sems,
):
    pos = pos_ref[0]
    late = pl.ds(ROWS, ROWS)
    fetch(
        ((pos == 0, kf_ref.at[late], vf_ref.at[late]), (pos != 0, k1_ref, v1_ref)),
        k_buf, wide1, sems,
    )
    set_ones(wide1)
    set_ones(wide0)
    for g in range(2):
        wide0[g, :, :HD] = v0_ref[:, g * HD : (g + 1) * HD]
    row = lax.broadcasted_iota(jnp.int32, (NEAR, NEAR), 0)
    col = lax.broadcasted_iota(jnp.int32, (NEAR, NEAR), 1)
    visible = col <= row
    for h in range(HEADS):
        g = h // RATIO
        mine = slice(h * HD, (h + 1) * HD)
        group = slice(g * HD, (g + 1) * HD)
        for i in range(ROWS // NEAR):
            lo, hi = i * NEAR, (i + 1) * NEAR
            q = q_ref[lo:hi, mine]
            parts = [(scores_of(q, k_buf[:, group]), wide1[g])]
            if i > 0:
                parts.append((scores_of(q, k0_ref[:lo, group]), wide0[g, :lo]))
            own = scores_of(q, k0_ref[lo:hi, group])
            parts.append((jnp.where(visible, own, -jnp.inf), wide0[g, lo:hi]))
            top = functools.reduce(
                jnp.maximum, [jnp.max(s, axis=1, keepdims=True) for s, _ in parts]
            )
            summed = jnp.zeros((NEAR, 2 * HD), jnp.float32)
            for s, values in parts:
                mass = jnp.exp2((s - top) * EXP_SCALE).astype(jnp.bfloat16)
                summed += jnp.dot(mass, values, preferred_element_type=jnp.float32)
            o_ref[lo:hi, mine] = summed[:, :HD]
            m_ref[lo:hi, h : h + 1] = top
            l_ref[lo:hi, h : h + 1] = summed[:, HD : HD + 1]


def block_scratch():
    return pltpu.VMEM((2, ROWS, 2 * HD), jnp.bfloat16)


def near(pos, q, k0, v0, k1, v1, kf, vf):
    stat = jax.ShapeDtypeStruct((ROWS, 128), jnp.float32)
    return pl.pallas_call(
        near_kernel,
        out_shape=(jax.ShapeDtypeStruct((ROWS, HEADS * HD), jnp.float32), stat, stat),
        in_specs=[smem(), vmem(), vmem(), vmem(), anywhere(), anywhere(), anywhere(), anywhere()],
        out_specs=(vmem(), vmem(), vmem()),
        scratch_shapes=[
            pltpu.VMEM((ROWS, WIDTH), jnp.bfloat16),
            block_scratch(),
            block_scratch(),
            pltpu.SemaphoreType.DMA((3,)),
        ],
        compiler_params=pltpu.CompilerParams(vmem_limit_bytes=LIMIT),
        cost_estimate=cost(3 << 30, 5 << 20),
        name="near",
    )(pos, q, k0, v0, k1, v1, kf, vf)


def far_kernel(
    pos_ref, q_ref, k2_ref, v2_ref, kf_ref, vf_ref, o_ref, m_ref, l_ref,
    out_ref, k_buf, wide, sems,
):
    pos = pos_ref[0]
    early = pl.ds(0, ROWS)
    late = pl.ds(ROWS, ROWS)
    set_ones(wide)
    fetch(
        (
            (pos == 0, kf_ref.at[early], vf_ref.at[early]),
            (pos == 1, kf_ref.at[late], vf_ref.at[late]),
            (pos > 1, k2_ref, v2_ref),
        ),
        k_buf, wide, sems,
    )
    for h in range(HEADS):
        g = h // RATIO
        mine = slice(h * HD, (h + 1) * HD)
        group = slice(g * HD, (g + 1) * HD)
        for i in range(ROWS // FAR):
            lo, hi = i * FAR, (i + 1) * FAR
            s = scores_of(q_ref[lo:hi, mine], k_buf[:, group])
            old_top = m_ref[lo:hi, h : h + 1]
            top = jnp.maximum(jnp.max(s, axis=1, keepdims=True), old_top)
            keep = jnp.exp2((old_top - top) * EXP_SCALE)
            mass = jnp.exp2((s - top) * EXP_SCALE).astype(jnp.bfloat16)
            summed = jnp.dot(mass, wide[g], preferred_element_type=jnp.float32)
            total = keep * l_ref[lo:hi, h : h + 1] + summed[:, HD:]
            out = (keep * o_ref[lo:hi, mine] + summed[:, :HD]) / total
            out_ref[lo:hi, mine] = out.astype(jnp.bfloat16)


def far(pos, q, k2, v2, kf, vf, o, m, l):
    return pl.pallas_call(
        far_kernel,
        out_shape=jax.ShapeDtypeStruct((ROWS, HEADS * HD), jnp.bfloat16),
        in_specs=[smem(), vmem(), anywhere(), anywhere(), anywhere(), anywhere(), vmem(), vmem(), vmem()],
        out_specs=vmem(),
        scratch_shapes=[
            pltpu.VMEM((ROWS, WIDTH), jnp.bfloat16),
            block_scratch(),
            pltpu.SemaphoreType.DMA((3,)),
        ],
        compiler_params=pltpu.CompilerParams(vmem_limit_bytes=LIMIT),
        cost_estimate=cost(2 << 30, 5 << 20),
        name="far",
    )(pos, q, k2, v2, kf, vf, o, m, l)


def shards(queries, keys_next, values_next, keys_front, values_front, keys_prev, values_prev):
    pos = lax.axis_index("seq").astype(jnp.int32).reshape(1)
    k1 = shifted(keys_next)
    v1 = shifted(values_next)
    k2 = shifted(k1)
    v2 = shifted(v1)
    packed = pack(keys_prev, values_prev)
    arrived = exchange(packed)
    state = near(pos, queries, keys_next, values_next, k1, v1, keys_front, values_front)
    attended = far(pos, queries, k2, v2, keys_front, values_front, *state)
    banded_keys, banded_values = unpack(arrived)
    return (attended, banded_keys, banded_values)


def solution(mesh):
    in_specs = (
        P("seq", "head"),
        P("seq", "head"),
        P("seq", "head"),
        P(None, "head"),
        P(None, "head"),
        P("seq", "head"),
        P("seq", "head"),
    )
    out_specs = (P("seq", "head"), P("seq", "head"), P("seq", "head"))
    return jax.shard_map(
        shards, mesh=mesh, in_specs=in_specs, out_specs=out_specs, check_vma=False
    )
```

```python
import jax
import jax.numpy as jnp
from jax import lax
from jax.experimental import pallas as pl
from jax.experimental.pallas import tpu as pltpu
from jax.sharding import PartitionSpec as P


QH = 32
KVH = 8
HD = 128
RATIO = QH // KVH
ROWS = 512
WIDTH = 256
HEADS = 8
RUN = 8
EXP_SCALE = 1.4426950408889634 * HD**-0.5
NEAR = 256
FAR = 256
LIMIT = 24 << 20


def shifted(value):
    count = lax.axis_size("seq")
    return lax.ppermute(value, "seq", [(source, source + 1) for source in range(count - 1)])


def crossing(value):
    count = lax.axis_size("seq")
    pairs = [(source, source + 2) for source in range(RUN - 2, count - 2, RUN)]
    return lax.ppermute(value, "seq", pairs)


def inner(value):
    count = lax.axis_size("seq")
    pairs = [(source, source + 1) for source in range(count) if source % RUN != RUN - 1]
    return lax.ppermute(value, "seq", pairs)


def vmem():
    return pl.BlockSpec(memory_space=pltpu.VMEM)


def anywhere():
    return pl.BlockSpec(memory_space=pl.ANY)


def smem():
    return pl.BlockSpec(memory_space=pltpu.SMEM)


def cost(flops, moved):
    return pl.CostEstimate(flops=flops, bytes_accessed=moved, transcendentals=0)


def chooser(size, source_of_row):
    row = lax.broadcasted_iota(jnp.int32, (size, size), 0)
    col = lax.broadcasted_iota(jnp.int32, (size, size), 1)
    return jnp.where(col == source_of_row(row), 1.0, 0.0).astype(jnp.bfloat16)


def moved_by(pick, parts):
    rows = jnp.concatenate(parts, axis=0) if len(parts) > 1 else parts[0]
    return jnp.dot(pick, rows, preferred_element_type=jnp.float32).astype(jnp.bfloat16)


def pack_kernel(k_ref, v_ref, out_ref):
    pick = chooser(128, lambda r: (r & 7) * 16 + (r >> 3))
    for c in range(8):
        out_ref[pl.ds(c * 128, 128), :] = moved_by(
            pick, [ref[pl.ds(k * 128 + c * 16, 16), :] for ref in (k_ref, v_ref) for k in range(4)])


def pack(keys, values):
    packed = pl.pallas_call(
        pack_kernel,
        out_shape=jax.ShapeDtypeStruct((2 * ROWS, WIDTH), jnp.bfloat16),
        in_specs=[vmem(), vmem()],
        out_specs=vmem(),
        cost_estimate=cost(1 << 26, 1 << 20),
        name="pack",
    )(keys, values)
    return packed.reshape(ROWS // 4, 8, WIDTH)


def unpack_kernel(x_ref, k_ref, v_ref):
    pick = chooser(128, lambda r: ((r >> 2) & 15) * 8 + (r >> 6) * 4 + (r & 3))
    for c in range(8):
        moved = moved_by(pick, [x_ref[pl.ds(c * 128, 128), :]])
        k_ref[pl.ds(c * 64, 64), :] = moved[:64]
        v_ref[pl.ds(c * 64, 64), :] = moved[64:]


def unpack(x):
    shape = jax.ShapeDtypeStruct((ROWS, WIDTH), jnp.bfloat16)
    return pl.pallas_call(
        unpack_kernel,
        out_shape=(shape, shape),
        in_specs=[vmem()],
        out_specs=(vmem(), vmem()),
        compiler_params=pltpu.CompilerParams(vmem_limit_bytes=8 << 20),
        cost_estimate=cost(1 << 26, 1 << 20),
        name="unpack",
    )(x.reshape(2 * ROWS, WIDTH))


def exchange(x):
    return lax.all_to_all(
        x, "seq", split_axis=0, concat_axis=0, tiled=True
    )


def scores_of(q, keys):
    return lax.dot_general(
        q, keys, (((1,), (1,)), ((), ())), preferred_element_type=jnp.float32
    )


def fetch(choices, sems):
    for when, moves in choices:

        @pl.when(when)
        def _(moves=moves):
            copies = [
                pltpu.make_async_copy(source, target, sems.at[n])
                for n, (source, target) in enumerate(moves)
            ]
            for copy in copies:
                copy.start()
            for copy in copies:
                copy.wait()


def set_ones(wide_buf):
    for g in range(2):
        wide_buf[g, :, HD:] = jnp.ones_like(wide_buf[g, :, HD:])


def widened(values_src, wide_buf):
    return [
        (values_src.at[:, pl.ds(g * HD, HD)], wide_buf.at[g, :, pl.ds(0, HD)]) for g in range(2)
    ]


def second_choices(pos, front, crossed, relayed):
    starts_run = lax.rem(pos, RUN) == 0
    return (
        (pos == 0, front.at[pl.ds(0, ROWS)]),
        (pos == 1, front.at[pl.ds(ROWS, ROWS)]),
        ((pos > 1) & starts_run, crossed),
        ((pos > 1) & jnp.logical_not(starts_run), relayed),
    )


def main_kernel(
    pos_ref, q_ref, k0_ref, v0_ref, k1_ref, v1_ref, k2_ref, kx_ref, kf_ref, vf_ref,
    o_ref, l_ref, p_ref, k1_buf, k2_buf, wide1, wide0, sems,
):
    pos = pos_ref[0]
    late = pl.ds(ROWS, ROWS)
    fetch(
        [
            (when, [(source, k2_buf)])
            for when, source in second_choices(pos, kf_ref, kx_ref, k2_ref)
        ],
        sems,
    )
    fetch(
        [
            (pos == 0, [(kf_ref.at[late], k1_buf)] + widened(vf_ref.at[late], wide1)),
            (pos != 0, [(k1_ref, k1_buf)] + widened(v1_ref, wide1)),
        ],
        sems,
    )
    set_ones(wide1)
    set_ones(wide0)
    for g in range(2):
        wide0[g, :, :HD] = v0_ref[:, g * HD : (g + 1) * HD]
    row = lax.broadcasted_iota(jnp.int32, (NEAR, NEAR), 0)
    col = lax.broadcasted_iota(jnp.int32, (NEAR, NEAR), 1)
    visible = col <= row
    for h in range(HEADS):
        g = h // RATIO
        mine = slice(h * HD, (h + 1) * HD)
        group = slice(g * HD, (g + 1) * HD)
        for i in range(ROWS // NEAR):
            lo, hi = i * NEAR, (i + 1) * NEAR
            q = q_ref[lo:hi, mine]
            second = scores_of(q, k2_buf[:, group])
            parts = [(scores_of(q, k1_buf[:, group]), wide1[g])]
            if i > 0:
                parts.append((scores_of(q, k0_ref[:lo, group]), wide0[g, :lo]))
            own = scores_of(q, k0_ref[lo:hi, group])
            parts.append((jnp.where(visible, own, -jnp.inf), wide0[g, lo:hi]))
            top = jnp.max(second, axis=1, keepdims=True)
            for s, _ in parts:
                top = jnp.maximum(top, jnp.max(s, axis=1, keepdims=True))
            p_ref[h, lo:hi, :] = jnp.exp2((second - top) * EXP_SCALE).astype(jnp.bfloat16)
            summed = jnp.zeros((NEAR, 2 * HD), jnp.float32)
            for s, values in parts:
                mass = jnp.exp2((s - top) * EXP_SCALE).astype(jnp.bfloat16)
                summed += jnp.dot(mass, values, preferred_element_type=jnp.float32)
            o_ref[lo:hi, mine] = summed[:, :HD]
            l_ref[lo:hi, h : h + 1] = summed[:, HD : HD + 1]


def block_scratch():
    return pltpu.VMEM((2, ROWS, 2 * HD), jnp.bfloat16)


def main(pos, q, k0, v0, k1, v1, k2, kx, kf, vf):
    return pl.pallas_call(
        main_kernel,
        out_shape=(
            jax.ShapeDtypeStruct((ROWS, HEADS * HD), jnp.float32),
            jax.ShapeDtypeStruct((ROWS, 128), jnp.float32),
            jax.ShapeDtypeStruct((HEADS, ROWS, ROWS), jnp.bfloat16),
        ),
        in_specs=[smem()] + [vmem()] * 3 + [anywhere()] * 6,
        out_specs=(vmem(), vmem(), vmem()),
        scratch_shapes=[
            pltpu.VMEM((ROWS, WIDTH), jnp.bfloat16),
            pltpu.VMEM((ROWS, WIDTH), jnp.bfloat16),
            block_scratch(),
            block_scratch(),
            pltpu.SemaphoreType.DMA((3,)),
        ],
        compiler_params=pltpu.CompilerParams(vmem_limit_bytes=LIMIT),
        cost_estimate=cost(5 << 30, 10 << 20),
        name="main",
    )(pos, q, k0, v0, k1, v1, k2, kx, kf, vf)


def last_kernel(pos_ref, o_ref, l_ref, p_ref, v2_ref, vx_ref, vf_ref, out_ref, wide, sems):
    pos = pos_ref[0]
    set_ones(wide)
    fetch(
        [
            (when, widened(source, wide))
            for when, source in second_choices(pos, vf_ref, vx_ref, v2_ref)
        ],
        sems,
    )
    for h in range(HEADS):
        mine = slice(h * HD, (h + 1) * HD)
        for i in range(ROWS // FAR):
            lo, hi = i * FAR, (i + 1) * FAR
            summed = jnp.dot(
                p_ref[h, lo:hi, :], wide[h // RATIO], preferred_element_type=jnp.float32
            )
            total = l_ref[lo:hi, h : h + 1] + summed[:, HD:]
            out = (o_ref[lo:hi, mine] + summed[:, :HD]) / total
            out_ref[lo:hi, mine] = out.astype(jnp.bfloat16)


def last(pos, o, l, p, v2, vx, vf):
    return pl.pallas_call(
        last_kernel,
        out_shape=jax.ShapeDtypeStruct((ROWS, HEADS * HD), jnp.bfloat16),
        in_specs=[smem()] + [vmem()] * 3 + [anywhere()] * 3,
        out_specs=vmem(),
        scratch_shapes=[block_scratch(), pltpu.SemaphoreType.DMA((2,))],
        compiler_params=pltpu.CompilerParams(vmem_limit_bytes=LIMIT),
        cost_estimate=cost(2 << 30, 5 << 20),
        name="last",
    )(pos, o, l, p, v2, vx, vf)


def shards(queries, keys_next, values_next, keys_front, values_front, keys_prev, values_prev):
    pos = lax.axis_index("seq").astype(jnp.int32).reshape(1)
    k1 = shifted(keys_next)
    v1 = shifted(values_next)
    kx = crossing(keys_next)
    vx = crossing(values_next)
    k2 = inner(k1)
    v2 = inner(v1)
    packed = pack(keys_prev, values_prev)
    arrived = exchange(packed)
    state = main(
        pos, queries, keys_next, values_next, k1, v1, k2, kx,
        keys_front, values_front,
    )
    attended = last(pos, *state, v2, vx, values_front)
    banded_keys, banded_values = unpack(arrived)
    return (attended, banded_keys, banded_values)


def solution(mesh):
    in_specs = (
        P("seq", "head"),
        P("seq", "head"),
        P("seq", "head"),
        P(None, "head"),
        P(None, "head"),
        P("seq", "head"),
        P("seq", "head"),
    )
    out_specs = (P("seq", "head"), P("seq", "head"), P("seq", "head"))
    return jax.shard_map(
        shards, mesh=mesh, in_specs=in_specs, out_specs=out_specs, check_vma=False
    )
```

```python
import jax
import jax.numpy as jnp
from jax import lax
from jax.experimental import pallas as pl
from jax.experimental.pallas import tpu as pltpu
from jax.sharding import PartitionSpec as P


QH = 32
KVH = 8
HD = 128
RATIO = QH // KVH
ROWS = 512
WIDTH = 256
HEADS = 8
RUN = 8
EXP_SCALE = 1.4426950408889634 * HD**-0.5
NEAR = 256
FAR = 256
LIMIT = 24 << 20


def shifted(value):
    count = lax.axis_size("seq")
    return lax.ppermute(value, "seq", [(source, source + 1) for source in range(count - 1)])


def crossing(value):
    count = lax.axis_size("seq")
    pairs = [(source, source + 2) for source in range(RUN - 2, count - 2, RUN)]
    return lax.ppermute(value, "seq", pairs)


def inner(value):
    count = lax.axis_size("seq")
    pairs = [(source, source + 1) for source in range(count) if source % RUN != RUN - 1]
    return lax.ppermute(value, "seq", pairs)


def vmem():
    return pl.BlockSpec(memory_space=pltpu.VMEM)


def anywhere():
    return pl.BlockSpec(memory_space=pl.ANY)


def smem():
    return pl.BlockSpec(memory_space=pltpu.SMEM)


def cost(flops, moved):
    return pl.CostEstimate(flops=flops, bytes_accessed=moved, transcendentals=0)


def chooser(size, source_of_row):
    row = lax.broadcasted_iota(jnp.int32, (size, size), 0)
    col = lax.broadcasted_iota(jnp.int32, (size, size), 1)
    return jnp.where(col == source_of_row(row), 1.0, 0.0).astype(jnp.bfloat16)


def moved_by(pick, parts):
    rows = jnp.concatenate(parts, axis=0) if len(parts) > 1 else parts[0]
    return jnp.dot(pick, rows, preferred_element_type=jnp.float32).astype(jnp.bfloat16)


def pack_kernel(k_ref, v_ref, out_ref):
    pick = chooser(128, lambda r: (r & 7) * 16 + (r >> 3))
    for c in range(8):
        out_ref[pl.ds(c * 128, 128), :] = moved_by(
            pick, [ref[pl.ds(k * 128 + c * 16, 16), :] for ref in (k_ref, v_ref) for k in range(4)])


def pack(keys, values):
    packed = pl.pallas_call(
        pack_kernel,
        out_shape=jax.ShapeDtypeStruct((2 * ROWS, WIDTH), jnp.bfloat16),
        in_specs=[vmem(), vmem()],
        out_specs=vmem(),
        cost_estimate=cost(1 << 26, 1 << 20),
        name="pack",
    )(keys, values)
    return packed.reshape(ROWS // 4, 8, WIDTH)


def unpack_kernel(x_ref, k_ref, v_ref, k_buf, v_buf, sems):
    pick = chooser(128, lambda r: ((r >> 2) & 15) * 8 + (r >> 6) * 4 + (r & 3))
    copies = []
    for c in range(8):
        moved = moved_by(pick, [x_ref[pl.ds(c * 128, 128), :]])
        k_buf[pl.ds(c * 64, 64), :] = moved[:64]
        v_buf[pl.ds(c * 64, 64), :] = moved[64:]
        if c % 2 == 1:
            span = pl.ds((c - 1) * 64, 128)
            for n, (buf, ref) in enumerate(((k_buf, k_ref), (v_buf, v_ref))):
                copy = pltpu.make_async_copy(buf.at[span], ref.at[span], sems.at[n, c // 2])
                copy.start()
                copies.append(copy)
    for copy in copies:
        copy.wait()


def unpack(x):
    shape = jax.ShapeDtypeStruct((ROWS, WIDTH), jnp.bfloat16)
    return pl.pallas_call(
        unpack_kernel,
        out_shape=(shape, shape),
        in_specs=[vmem()],
        out_specs=(anywhere(), anywhere()),
        scratch_shapes=[
            pltpu.VMEM((ROWS, WIDTH), jnp.bfloat16),
            pltpu.VMEM((ROWS, WIDTH), jnp.bfloat16),
            pltpu.SemaphoreType.DMA((2, 4)),
        ],
        compiler_params=pltpu.CompilerParams(vmem_limit_bytes=8 << 20),
        cost_estimate=cost(1 << 26, 1 << 20),
        name="unpack",
    )(x.reshape(2 * ROWS, WIDTH))


def exchange(x):
    return lax.all_to_all(
        x, "seq", split_axis=0, concat_axis=0, tiled=True
    )


def scores_of(q, keys):
    return lax.dot_general(
        q, keys, (((1,), (1,)), ((), ())), preferred_element_type=jnp.float32
    )


def fetch(choices, sems):
    for when, moves in choices:

        @pl.when(when)
        def _(moves=moves):
            copies = [
                pltpu.make_async_copy(source, target, sems.at[n])
                for n, (source, target) in enumerate(moves)
            ]
            for copy in copies:
                copy.start()
            for copy in copies:
                copy.wait()


def set_ones(wide_buf):
    for g in range(2):
        wide_buf[g, :, HD:] = jnp.ones_like(wide_buf[g, :, HD:])


def widened(values_src, wide_buf):
    return [
        (values_src.at[:, pl.ds(g * HD, HD)], wide_buf.at[g, :, pl.ds(0, HD)]) for g in range(2)
    ]


def second_choices(pos, front, crossed, relayed):
    starts_run = lax.rem(pos, RUN) == 0
    return (
        (pos == 0, front.at[pl.ds(0, ROWS)]),
        (pos == 1, front.at[pl.ds(ROWS, ROWS)]),
        ((pos > 1) & starts_run, crossed),
        ((pos > 1) & jnp.logical_not(starts_run), relayed),
    )


def main_kernel(
    pos_ref, q_ref, k0_ref, v0_ref, k1_ref, v1_ref, k2_ref, kx_ref, kf_ref, vf_ref,
    o_ref, l_ref, p_ref, k1_buf, k2_buf, wide1, wide0, sems,
):
    pos = pos_ref[0]
    late = pl.ds(ROWS, ROWS)
    fetch(
        [
            (when, [(source, k2_buf)])
            for when, source in second_choices(pos, kf_ref, kx_ref, k2_ref)
        ],
        sems,
    )
    fetch(
        [
            (pos == 0, [(kf_ref.at[late], k1_buf)] + widened(vf_ref.at[late], wide1)),
            (pos != 0, [(k1_ref, k1_buf)] + widened(v1_ref, wide1)),
        ],
        sems,
    )
    set_ones(wide1)
    set_ones(wide0)
    for g in range(2):
        wide0[g, :, :HD] = v0_ref[:, g * HD : (g + 1) * HD]
    row = lax.broadcasted_iota(jnp.int32, (NEAR, NEAR), 0)
    col = lax.broadcasted_iota(jnp.int32, (NEAR, NEAR), 1)
    visible = col <= row
    for h in range(HEADS):
        g = h // RATIO
        mine = slice(h * HD, (h + 1) * HD)
        group = slice(g * HD, (g + 1) * HD)
        for i in range(ROWS // NEAR):
            lo, hi = i * NEAR, (i + 1) * NEAR
            q = q_ref[lo:hi, mine]
            second = scores_of(q, k2_buf[:, group])
            parts = [(scores_of(q, k1_buf[:, group]), wide1[g])]
            if i > 0:
                parts.append((scores_of(q, k0_ref[:lo, group]), wide0[g, :lo]))
            own = scores_of(q, k0_ref[lo:hi, group])
            parts.append((jnp.where(visible, own, -jnp.inf), wide0[g, lo:hi]))
            top = jnp.max(second, axis=1, keepdims=True)
            for s, _ in parts:
                top = jnp.maximum(top, jnp.max(s, axis=1, keepdims=True))
            p_ref[h, lo:hi, :] = jnp.exp2((second - top) * EXP_SCALE).astype(jnp.bfloat16)
            summed = jnp.zeros((NEAR, 2 * HD), jnp.float32)
            for s, values in parts:
                mass = jnp.exp2((s - top) * EXP_SCALE).astype(jnp.bfloat16)
                summed += jnp.dot(mass, values, preferred_element_type=jnp.float32)
            o_ref[lo:hi, mine] = summed[:, :HD]
            l_ref[lo:hi, h : h + 1] = summed[:, HD : HD + 1]


def block_scratch():
    return pltpu.VMEM((2, ROWS, 2 * HD), jnp.bfloat16)


def main(pos, q, k0, v0, k1, v1, k2, kx, kf, vf):
    return pl.pallas_call(
        main_kernel,
        out_shape=(
            jax.ShapeDtypeStruct((ROWS, HEADS * HD), jnp.float32),
            jax.ShapeDtypeStruct((ROWS, 128), jnp.float32),
            jax.ShapeDtypeStruct((HEADS, ROWS, ROWS), jnp.bfloat16),
        ),
        in_specs=[smem()] + [vmem()] * 3 + [anywhere()] * 6,
        out_specs=(vmem(), vmem(), vmem()),
        scratch_shapes=[
            pltpu.VMEM((ROWS, WIDTH), jnp.bfloat16),
            pltpu.VMEM((ROWS, WIDTH), jnp.bfloat16),
            block_scratch(),
            block_scratch(),
            pltpu.SemaphoreType.DMA((3,)),
        ],
        compiler_params=pltpu.CompilerParams(vmem_limit_bytes=LIMIT),
        cost_estimate=cost(5 << 30, 10 << 20),
        name="main",
    )(pos, q, k0, v0, k1, v1, k2, kx, kf, vf)


def last_kernel(
    pos_ref, o_ref, l_ref, p_ref, v2_ref, vx_ref, vf_ref, out_ref, wide, out_buf, sems, out_sems
):
    pos = pos_ref[0]
    set_ones(wide)
    fetch(
        [
            (when, widened(source, wide))
            for when, source in second_choices(pos, vf_ref, vx_ref, v2_ref)
        ],
        sems,
    )
    copies = []
    for h in range(HEADS):
        mine = slice(h * HD, (h + 1) * HD)
        for i in range(ROWS // FAR):
            lo, hi = i * FAR, (i + 1) * FAR
            summed = jnp.dot(
                p_ref[h, lo:hi, :], wide[h // RATIO], preferred_element_type=jnp.float32
            )
            total = l_ref[lo:hi, h : h + 1] + summed[:, HD:]
            out = (o_ref[lo:hi, mine] + summed[:, :HD]) / total
            out_buf[lo:hi, mine] = out.astype(jnp.bfloat16)
        if h % 2 == 1:
            pair = pl.ds((h - 1) * HD, 2 * HD)
            copy = pltpu.make_async_copy(
                out_buf.at[:, pair], out_ref.at[:, pair], out_sems.at[h // 2]
            )
            copy.start()
            copies.append(copy)
    for copy in copies:
        copy.wait()


def last(pos, o, l, p, v2, vx, vf):
    return pl.pallas_call(
        last_kernel,
        out_shape=jax.ShapeDtypeStruct((ROWS, HEADS * HD), jnp.bfloat16),
        in_specs=[smem()] + [vmem()] * 3 + [anywhere()] * 3,
        out_specs=anywhere(),
        scratch_shapes=[
            block_scratch(),
            pltpu.VMEM((ROWS, HEADS * HD), jnp.bfloat16),
            pltpu.SemaphoreType.DMA((2,)),
            pltpu.SemaphoreType.DMA((HEADS // 2,)),
        ],
        compiler_params=pltpu.CompilerParams(vmem_limit_bytes=LIMIT),
        cost_estimate=cost(2 << 30, 5 << 20),
        name="last",
    )(pos, o, l, p, v2, vx, vf)


def shards(queries, keys_next, values_next, keys_front, values_front, keys_prev, values_prev):
    pos = lax.axis_index("seq").astype(jnp.int32).reshape(1)
    k1 = shifted(keys_next)
    v1 = shifted(values_next)
    kx = crossing(keys_next)
    vx = crossing(values_next)
    k2 = inner(k1)
    v2 = inner(v1)
    packed = pack(keys_prev, values_prev)
    arrived = exchange(packed)
    state = main(
        pos, queries, keys_next, values_next, k1, v1, k2, kx,
        keys_front, values_front,
    )
    attended = last(pos, *state, v2, vx, values_front)
    banded_keys, banded_values = unpack(arrived)
    return (attended, banded_keys, banded_values)


def solution(mesh):
    in_specs = (
        P("seq", "head"),
        P("seq", "head"),
        P("seq", "head"),
        P(None, "head"),
        P(None, "head"),
        P("seq", "head"),
        P("seq", "head"),
    )
    out_specs = (P("seq", "head"), P("seq", "head"), P("seq", "head"))
    return jax.shard_map(
        shards, mesh=mesh, in_specs=in_specs, out_specs=out_specs, check_vma=False
    )
```
